32 devices in a mesh: seq: 4 (over y, x), grp: 2 (over core), wsh: 4 (over z).
Axes of the slice: x: 2, y: 2, z: 4, core: 2. Of those that a mesh axis runs over, the one named last changes fastest.
Arguments:
- hidden: bfloat16 [8, 1024, 1536], P(('grp', 'wsh'), 'seq'), may hold values from -6 to 6
- norm_gain: bfloat16 [1536], P('wsh'), may hold values from 0.5 to 1.5
- in_weight: bfloat16 [1536, 6448], P('wsh'), may hold values from -0.15625 to 0.15625
- conv_weight: bfloat16 [3328, 4], P('wsh'), may hold values from -3 to 3
- conv_bias: bfloat16 [3328], P('wsh'), may hold values from -3 to 3
- dt_bias: bfloat16 [48], P('wsh'), may hold values from -13 to -3
- a_log: bfloat16 [48], P('wsh'), may hold values from 0 to 2.7
- skip_gain: bfloat16 [48], P('wsh'), may hold values from 0.5 to 2
- gate_gain: bfloat16 [3072], P('wsh'), may hold values from 0.5 to 1.5
- out_weight: bfloat16 [3072, 1536], P('wsh'), may hold values from -0.109375 to 0.109375
- d_out: bfloat16 [8, 1024, 1536], P(('grp', 'wsh'), 'seq'), may hold values from -6 to 6
Outputs:
- layer_out: bfloat16 [8, 1024, 1536], P(('grp', 'wsh'), 'seq')
- d_hidden: bfloat16 [8, 1024, 1536], P(('grp', 'wsh'), 'seq')
- grad_norm_gain: float32 [1536], P('wsh')
- grad_in_weight: float32 [1536, 6448], P('wsh')
- grad_conv_weight: float32 [3328, 4], P('wsh')
- grad_conv_bias: float32 [3328], P('wsh')
- grad_dt_bias: float32 [48], P('wsh')
- grad_a_log: float32 [48], P('wsh')
- grad_skip_gain: float32 [48], P('wsh')
- grad_gate_gain: float32 [3072], P('wsh')
- grad_out_weight: float32 [3072, 1536], P('wsh')
The draws below stay inside these ranges and needn't reach their ends.
All inputs are finite; a program needn't handle non-finite values.
Results may differ from the reference program's by a relative error of at most 0.0091.
Values may be sent and summed in bfloat16 or wider, within the bound.
No kernel may reach another device: no remote copies, remote signals or barrier semaphores. Data moves between devices by JAX's collectives and lax.ppermute only.
A program may use at most 320 MiB of HBM per device.

```python
import math
import jax
import jax.numpy as jnp
from jax import lax

D = 1536
DI = 3072
HEADS = 48
KCONV = 4
QCH = 256
SEQLEN = 1024
SEQS = 8
CONVC = 3328
PROJ = 6448
N_SEQ = 4


def head_laws(key):
    slow_share = 0.5
    least_decay = 0.3
    pick_key = jax.random.fold_in(key, 7101)
    slow_rate_key = jax.random.fold_in(key, 7102)
    fast_rate_key = jax.random.fold_in(key, 7103)
    total_key = jax.random.fold_in(key, 7104)
    window_key = jax.random.fold_in(key, 7105)
    slow_mask = jax.random.uniform(pick_key, (HEADS,), jnp.float32) < slow_share
    slow_alog = jax.random.uniform(slow_rate_key, (HEADS,), jnp.float32, 0.0, 1.0)
    fast_alog = jax.random.uniform(fast_rate_key, (HEADS,), jnp.float32, 0.0, 2.7)
    alog_values = jnp.where(slow_mask, slow_alog, fast_alog)
    total_decay = jnp.exp(jax.random.uniform(total_key, (HEADS,), jnp.float32, math.log(least_decay), math.log(2.0)))
    window = jnp.exp(jax.random.uniform(window_key, (HEADS,), jnp.float32, math.log(20.0), math.log(60.0)))
    slow_bias = jnp.log(total_decay / (1.65 * SEQLEN)) - alog_values
    fast_bias = jnp.log(1.0 / (1.65 * window)) - alog_values
    bias_values = jnp.where(slow_mask, slow_bias, fast_bias)
    return (alog_values, bias_values)


def draw_dt_bias(key, part):
    return head_laws(key)[1].astype(jnp.bfloat16)


def draw_a_log(key, part):
    return head_laws(key)[0].astype(jnp.bfloat16)


def strengthened(drawn, stream_key, source, target, parts, factor):
    def block_of(position):
        return (jnp.arange(drawn.shape[position]) // (drawn.shape[position] // parts)).reshape((-1,) + (1,) * (drawn.ndim - 1 - position))

    one_side = jax.random.permutation(stream_key, parts)[block_of(target)]
    second = (block_of(target) + parts // 2) % parts
    return jnp.where((block_of(source) == one_side) | (block_of(source) == second), factor * drawn, drawn)


def block_levels(own_key, shape, split, least, high):
    loudness = 1.0
    for axis_at, parts in split:
        steps = jax.random.uniform(jax.random.fold_in(jax.random.fold_in(own_key, 6), axis_at), (parts,), jnp.float32, least / len(split), high / len(split))
        loudness = loudness * jnp.repeat(jnp.exp(steps), shape[axis_at] // parts).reshape((-1,) + (1,) * (len(shape) - 1 - axis_at))
    return loudness


def normal_values(stream_key, shape, width, bound, cuts=(), dtype=jnp.bfloat16):
    drawn = width * jax.random.normal(stream_key, shape, jnp.float32)
    if cuts:
        drawn = drawn * block_levels(stream_key, shape, cuts, -0.22, 0.18)
    return jnp.clip(drawn, -bound, bound).astype(dtype)


def bell_draw_with(key, dims, scale, bound, shards, heavy, kind=jnp.bfloat16):
    entries = scale * jax.random.normal(key, dims, jnp.float32)
    if shards:
        entries = entries * block_levels(key, dims, shards, -0.22, 0.18)
    return jnp.clip(strengthened(entries, jax.random.fold_in(key, 3), *heavy), -bound, bound).astype(kind)


def setup_inputs(seed: int = 0) -> dict:
    key_list = jax.random.split(jax.random.key(seed), 12)
    return {
        "hidden": bell_draw_with(key_list[0], (SEQS, SEQLEN, D), 1.0, 6.0, ((0, 8), (1, 4)), (1, 2, 4, 2.0)),
        "norm_gain": jnp.clip(1.0 + 0.1 * jax.random.normal(key_list[1], (D,), jnp.float32), 0.5, 1.5).astype(jnp.bfloat16),
        "in_weight": normal_values(key_list[2], (D, PROJ), D ** -0.5, 0.15625, ((0, 4),)),
        "conv_weight": normal_values(key_list[3], (CONVC, KCONV), KCONV ** -0.5, 3.0, ((0, 4),)),
        "conv_bias": normal_values(key_list[4], (CONVC,), 0.5, 3.0, ((0, 4),)),
        "dt_bias": draw_dt_bias(jax.random.fold_in(key_list[11], 71), 0),
        "a_log": draw_a_log(jax.random.fold_in(key_list[11], 71), 0),
        "skip_gain": jnp.clip(0.5 + 1.5 * jax.random.uniform(key_list[7], (HEADS,), jnp.float32) ** block_levels(key_list[7], (HEADS,), ((0, 4),), -0.2, 0.2), 0.5, 2.0).astype(jnp.bfloat16),
        "gate_gain": jnp.clip(1.0 + 0.1 * jax.random.normal(key_list[8], (DI,), jnp.float32), 0.5, 1.5).astype(jnp.bfloat16),
        "out_weight": normal_values(key_list[9], (DI, D), DI ** -0.5, 0.109375, ((0, 4),)),
        "d_out": bell_draw_with(key_list[10], (SEQS, SEQLEN, D), 1.0, 6.0, ((0, 8), (1, 4)), (1, 2, 4, 2.0)),
    }


epsilon = 1e-05
highest = lax.Precision.HIGHEST

def rms_apply(values, gain_vec):
    inverse = lax.rsqrt(lax.optimization_barrier(jnp.mean(values * values, axis=-1, keepdims=True)) + epsilon)
    return values * inverse * gain_vec[None, :]

def gated_apply(mixer_out, gate_in, gain_vec):
    product = mixer_out * jax.nn.silu(gate_in)
    inverse = lax.rsqrt(lax.optimization_barrier(jnp.mean(product * product, axis=-1, keepdims=True)) + epsilon)
    return product * inverse * gain_vec[None, :]

def conv_apply(padded, weight, bias_vec):
    tap_count = weight.shape[1]
    row_count = padded.shape[0] - tap_count + 1
    summed = jnp.zeros((row_count, padded.shape[1]), jnp.float32) + bias_vec[None, :]
    for offset in range(tap_count):
        summed = summed + padded[offset:offset + row_count] * weight[:, offset][None, :]
    return jax.nn.silu(summed)

def ssd_apply(x_values, dt_raw, b_and_c, dt_bias, a_log, skip_gain):
    length, head_count = dt_raw.shape
    head_size = x_values.shape[1] // head_count
    state_count = b_and_c.shape[1] // 2
    block_count = length // QCH
    dt_value = jax.nn.softplus(dt_raw + dt_bias[None, :])
    log_rate = -jnp.exp(a_log)[None, :] * dt_value
    causal = (jnp.arange(QCH)[:, None] >= jnp.arange(QCH)[None, :]).astype(jnp.float32)
    x_blocks = x_values.reshape(block_count, QCH, head_count, head_size)
    dt_blocks = dt_value.reshape(block_count, QCH, head_count)
    rate_blocks = log_rate.reshape(block_count, QCH, head_count)
    b_blocks = b_and_c[:, :state_count].reshape(block_count, QCH, state_count)
    c_blocks = b_and_c[:, state_count:].reshape(block_count, QCH, state_count)

    def advance(carried, pieces):
        x_block, dt_block, rate_block, b_block, c_block = pieces
        cumulated = jnp.cumsum(rate_block, axis=0)
        gram_matrix = jnp.dot(c_block, b_block.T, precision=highest)
        spread = cumulated.T[:, :, None] - cumulated.T[:, None, :]
        mixing = jnp.exp(spread * causal[None]) * causal[None] * gram_matrix[None] * dt_block.T[:, None, :]
        result = jnp.einsum('hts,shp->thp', mixing, x_block, precision=highest)
        result = result + jnp.einsum('tn,hnp->thp', c_block, carried, precision=highest) * jnp.exp(cumulated)[:, :, None]
        final_sum = cumulated[-1]
        tail_weight = jnp.exp(final_sum[None, :] - cumulated) * dt_block
        carried = carried * jnp.exp(final_sum)[:, None, None] + jnp.einsum('sn,sh,shp->hnp', b_block, tail_weight, x_block, precision=highest)
        return (carried, result)
    initial = jnp.zeros((head_count, state_count, head_size), jnp.float32)
    _, outputs = lax.scan(advance, initial, (x_blocks, dt_blocks, rate_blocks, b_blocks, c_blocks))
    return outputs.reshape(length, head_count * head_size) + x_values * jnp.repeat(skip_gain, head_size)[None, :]

def one_sequence(hidden_row, cotangent, params):
    norm_gain, in_weight, conv_weight, conv_bias, dt_bias, a_log, skip_gain, gate_gain, out_weight = params
    tokens_f = hidden_row.astype(jnp.float32)
    normed_f, rms_back = jax.vjp(rms_apply, tokens_f, norm_gain.astype(jnp.float32))
    normed = lax.optimization_barrier(normed_f.astype(jnp.bfloat16))
    projected = lax.optimization_barrier(jnp.dot(normed, in_weight, preferred_element_type=jnp.float32).astype(jnp.bfloat16))
    gate_part = projected[:, :DI]
    conv_input = projected[:, DI:DI + CONVC]
    dt_part = projected[:, DI + CONVC:]
    padded = jnp.concatenate([jnp.zeros((KCONV - 1, CONVC), jnp.bfloat16), conv_input], axis=0).astype(jnp.float32)
    conved_f, conv_back = jax.vjp(conv_apply, padded, conv_weight.astype(jnp.float32), conv_bias.astype(jnp.float32))
    conved = lax.optimization_barrier(conved_f.astype(jnp.bfloat16))
    x_groups = conved[:, :DI].astype(jnp.float32).reshape(SEQLEN, N_SEQ, DI // N_SEQ).transpose(1, 0, 2)
    dt_groups = dt_part.astype(jnp.float32).reshape(SEQLEN, N_SEQ, HEADS // N_SEQ).transpose(1, 0, 2)
    b_and_c = conved[:, DI:].astype(jnp.float32)
    head_params = (dt_bias.astype(jnp.float32).reshape(N_SEQ, HEADS // N_SEQ), a_log.astype(jnp.float32).reshape(N_SEQ, HEADS // N_SEQ), skip_gain.astype(jnp.float32).reshape(N_SEQ, HEADS // N_SEQ))

    def forward_group(pieces):
        return ssd_apply(pieces[0], pieces[1], b_and_c, pieces[2], pieces[3], pieces[4]).astype(jnp.bfloat16)
    y_groups = lax.map(forward_group, (x_groups, dt_groups) + head_params)
    y_rounded = lax.optimization_barrier(y_groups.transpose(1, 0, 2).reshape(SEQLEN, DI))
    gated_f, gate_back = jax.vjp(gated_apply, y_rounded.astype(jnp.float32), gate_part.astype(jnp.float32), gate_gain.astype(jnp.float32))
    gated = gated_f.astype(jnp.bfloat16)
    layer_out = (tokens_f + jnp.dot(gated, out_weight, preferred_element_type=jnp.float32)).astype(jnp.bfloat16)
    grad_out = jnp.dot(gated.T, cotangent, preferred_element_type=jnp.float32)
    d_gated = jnp.dot(cotangent, out_weight.T, preferred_element_type=jnp.float32)
    d_mixer, d_gate_part, grad_gate = gate_back(d_gated)
    d_y_rounded = lax.optimization_barrier(d_mixer.astype(jnp.bfloat16)).astype(jnp.float32)
    d_y_groups = d_y_rounded.reshape(SEQLEN, N_SEQ, DI // N_SEQ).transpose(1, 0, 2)

    def backward_group(pieces):
        _, ssd_back = jax.vjp(ssd_apply, pieces[0], pieces[1], b_and_c, pieces[2], pieces[3], pieces[4])
        return ssd_back(pieces[5])
    d_x, d_dt, d_bc, grad_dtb, grad_alog, grad_skip = lax.map(backward_group, (x_groups, dt_groups) + head_params + (d_y_groups,))
    d_x_rounded = lax.optimization_barrier(d_x.transpose(1, 0, 2).reshape(SEQLEN, DI).astype(jnp.bfloat16))
    d_dt_rounded = lax.optimization_barrier(d_dt.transpose(1, 0, 2).reshape(SEQLEN, HEADS).astype(jnp.bfloat16))
    d_conved = jnp.concatenate([d_x_rounded.astype(jnp.float32), lax.optimization_barrier(jnp.sum(d_bc, axis=0))], axis=1)
    d_padded, grad_conv, grad_cbias = conv_back(d_conved)
    d_projected = jnp.concatenate([d_gate_part, d_padded[KCONV - 1:], d_dt_rounded.astype(jnp.float32)], axis=1).astype(jnp.bfloat16)
    grad_in = jnp.dot(normed.T, d_projected, preferred_element_type=jnp.float32)
    d_normed = jnp.dot(d_projected, in_weight.T, preferred_element_type=jnp.float32)
    d_tokens, grad_norm = rms_back(d_normed)
    d_hidden = (cotangent.astype(jnp.float32) + d_tokens).astype(jnp.bfloat16)
    grads = (grad_norm, grad_in, grad_conv, grad_cbias, grad_dtb.reshape(HEADS), grad_alog.reshape(HEADS), grad_skip.reshape(HEADS), grad_gate, grad_out)
    return (layer_out, d_hidden, grads)

def reference(hidden, norm_gain, in_weight, conv_weight, conv_bias, dt_bias, a_log, skip_gain, gate_gain, out_weight, d_out):
    params = (norm_gain, in_weight, conv_weight, conv_bias, dt_bias, a_log, skip_gain, gate_gain, out_weight)
    zero_grads = tuple((jnp.zeros(weight.shape, jnp.float32) for weight in params))

    def accumulate(carried, pieces):
        layer_row, d_row, grads = one_sequence(pieces[0], pieces[1], params)
        return (tuple((first + second for first, second in zip(carried, grads))), (layer_row, d_row))
    totals, stacked = lax.scan(accumulate, zero_grads, (hidden, d_out))
    return (stacked[0], stacked[1], totals[0], totals[1], totals[2], totals[3], totals[4], totals[5], totals[6], totals[7], totals[8])
```

```python
import functools

import jax
import jax.numpy as jnp
from jax import lax
from jax.experimental import pallas as pl
from jax.experimental.pallas import tpu as pltpu
from jax.sharding import PartitionSpec as P

DI = 3072
KCONV = 4
QCH = 256
CONVC = 3328


epsilon = 1e-05
highest = lax.Precision.HIGHEST


def shifted(block, axis, distance):
    devices = range(lax.axis_size(axis))
    route = [(i - distance, i) for i in devices if i - distance in devices]
    return lax.ppermute(block, axis, route)


def rms_apply(values, gain_vec):
    inverse = lax.rsqrt(jnp.mean(values * values, axis=-1, keepdims=True) + epsilon)
    return values * inverse * gain_vec[None, :]


def gated_apply(mixer_out, gate_in, gain_vec):
    product = mixer_out * jax.nn.silu(gate_in)
    inverse = lax.rsqrt(jnp.mean(product * product, axis=-1, keepdims=True) + epsilon)
    return product * inverse * gain_vec[None, :]


def conv_apply(padded, weight, bias_vec):
    tap_count = weight.shape[1]
    row_count = padded.shape[0] - tap_count + 1
    summed = jnp.zeros((row_count, padded.shape[1]), jnp.float32) + bias_vec[None, :]
    for offset in range(tap_count):
        summed = summed + padded[offset : offset + row_count] * weight[:, offset][None, :]
    return jax.nn.silu(summed)


def ssd_apply(x_values, dt_raw, b_and_c, dt_bias, a_log, skip_gain):
    length, head_count = dt_raw.shape
    head_size = x_values.shape[1] // head_count
    state_count = b_and_c.shape[1] // 2
    block_count = length // QCH
    dt_value = jax.nn.softplus(dt_raw + dt_bias[None, :])
    log_rate = -jnp.exp(a_log)[None, :] * dt_value
    causal = (jnp.arange(QCH)[:, None] >= jnp.arange(QCH)[None, :]).astype(jnp.float32)
    x_blocks = x_values.reshape(block_count, QCH, head_count, head_size)
    dt_blocks = dt_value.reshape(block_count, QCH, head_count)
    rate_blocks = log_rate.reshape(block_count, QCH, head_count)
    b_blocks = b_and_c[:, :state_count].reshape(block_count, QCH, state_count)
    c_blocks = b_and_c[:, state_count:].reshape(block_count, QCH, state_count)

    def advance(carried, pieces):
        x_block, dt_block, rate_block, b_block, c_block = pieces
        cumulated = jnp.cumsum(rate_block, axis=0)
        gram_matrix = jnp.dot(c_block, b_block.T, precision=highest)
        spread = cumulated.T[:, :, None] - cumulated.T[:, None, :]
        mixing = (
            jnp.exp(spread * causal[None])
            * causal[None]
            * gram_matrix[None]
            * dt_block.T[:, None, :]
        )
        result = jnp.einsum("hts,shp->thp", mixing, x_block, precision=highest)
        result = (
            result
            + jnp.einsum("tn,hnp->thp", c_block, carried, precision=highest)
            * jnp.exp(cumulated)[:, :, None]
        )
        final_sum = cumulated[-1]
        tail_weight = jnp.exp(final_sum[None, :] - cumulated) * dt_block
        carried = carried * jnp.exp(final_sum)[:, None, None] + jnp.einsum(
            "sn,sh,shp->hnp", b_block, tail_weight, x_block, precision=highest
        )
        return (carried, result)

    initial = jnp.zeros((head_count, state_count, head_size), jnp.float32)
    _, outputs = lax.scan(advance, initial, (x_blocks, dt_blocks, rate_blocks, b_blocks, c_blocks))
    return (
        outputs.reshape(length, head_count * head_size)
        + x_values * jnp.repeat(skip_gain, head_size)[None, :]
    )


def reduce_grads(grads):
    shares = (
        lax.psum_scatter(grads[0], "wsh", scatter_dimension=0, tiled=True),
        lax.psum_scatter(grads[1], "wsh", scatter_dimension=0, tiled=True),
        lax.psum_scatter(grads[2], "wsh", scatter_dimension=0, tiled=True),
        lax.psum_scatter(grads[3], "wsh", scatter_dimension=0, tiled=True),
        lax.psum_scatter(grads[4], "wsh", scatter_dimension=0, tiled=True),
        lax.psum_scatter(grads[5], "wsh", scatter_dimension=0, tiled=True),
        lax.psum_scatter(grads[6], "wsh", scatter_dimension=0, tiled=True),
        lax.psum_scatter(grads[7], "wsh", scatter_dimension=0, tiled=True),
        lax.psum_scatter(grads[8], "wsh", scatter_dimension=0, tiled=True),
    )
    return lax.psum(
        (
            shares[0],
            shares[1],
            shares[2],
            shares[3],
            shares[4],
            shares[5],
            shares[6],
            shares[7],
            shares[8],
        ),
        ("seq", "grp"),
    )


def token_parallel_body(
    hidden,
    norm_gain,
    in_weight,
    conv_weight,
    conv_bias,
    dt_bias,
    a_log,
    skip_gain,
    gate_gain,
    out_weight,
    d_out,
):
    gathered = (
        lax.all_gather(norm_gain, "wsh", axis=0, tiled=True),
        lax.all_gather(in_weight, "wsh", axis=0, tiled=True),
        lax.all_gather(conv_weight, "wsh", axis=0, tiled=True),
        lax.all_gather(conv_bias, "wsh", axis=0, tiled=True),
        lax.all_gather(dt_bias, "wsh", axis=0, tiled=True),
        lax.all_gather(a_log, "wsh", axis=0, tiled=True),
        lax.all_gather(skip_gain, "wsh", axis=0, tiled=True),
    )
    full_norm, full_in, full_conv, full_cbias, full_dtb, full_alog, full_skip = gathered
    tokens_f = hidden[0].astype(jnp.float32)
    cotangent = d_out[0]
    normed_f, rms_back = jax.vjp(rms_apply, tokens_f, full_norm.astype(jnp.float32))
    normed = lax.optimization_barrier(normed_f.astype(jnp.bfloat16))
    projected = lax.optimization_barrier(
        jnp.dot(normed, full_in, preferred_element_type=jnp.float32).astype(jnp.bfloat16)
    )
    gate_part = projected[:, :DI]
    conv_input = projected[:, DI : DI + CONVC]
    dt_part = projected[:, DI + CONVC :]
    rim_rows = shifted(conv_input[conv_input.shape[0] - (KCONV - 1) :], "seq", 1)
    padded = jnp.concatenate([rim_rows, conv_input], axis=0).astype(jnp.float32)
    conved_f, conv_back = jax.vjp(
        conv_apply, padded, full_conv.astype(jnp.float32), full_cbias.astype(jnp.float32)
    )
    conved = lax.optimization_barrier(conved_f.astype(jnp.bfloat16))
    x_heads, dt_heads = (
        lax.all_to_all(conved[:, :DI], "seq", split_axis=1, concat_axis=0, tiled=True),
        lax.all_to_all(dt_part, "seq", split_axis=1, concat_axis=0, tiled=True),
    )
    bc_whole = lax.all_gather(conved[:, DI:], "seq", axis=0, tiled=True)
    local_heads = dt_heads.shape[1]
    head_start = lax.axis_index("seq") * local_heads
    bias_local = lax.dynamic_slice_in_dim(full_dtb.astype(jnp.float32), head_start, local_heads)
    alog_local = lax.dynamic_slice_in_dim(full_alog.astype(jnp.float32), head_start, local_heads)
    skip_local = lax.dynamic_slice_in_dim(full_skip.astype(jnp.float32), head_start, local_heads)
    x_float = x_heads.astype(jnp.float32)
    dt_float = dt_heads.astype(jnp.float32)
    bc_float = bc_whole.astype(jnp.float32)
    y_heads = ssd_apply(x_float, dt_float, bc_float, bias_local, alog_local, skip_local).astype(
        jnp.bfloat16
    )
    y_tokens = lax.all_to_all(y_heads, "seq", split_axis=0, concat_axis=1, tiled=True)
    full_gate, full_out = (
        lax.all_gather(gate_gain, "wsh", axis=0, tiled=True),
        lax.all_gather(out_weight, "wsh", axis=0, tiled=True),
    )
    gated_f, gate_back = jax.vjp(
        gated_apply,
        y_tokens.astype(jnp.float32),
        gate_part.astype(jnp.float32),
        full_gate.astype(jnp.float32),
    )
    gated = gated_f.astype(jnp.bfloat16)
    layer_out = (tokens_f + jnp.dot(gated, full_out, preferred_element_type=jnp.float32)).astype(
        jnp.bfloat16
    )
    grad_out = jnp.einsum("td,te->de", gated, cotangent, preferred_element_type=jnp.float32)
    d_gated = lax.dot_general(
        cotangent, full_out, (((1,), (1,)), ((), ())), preferred_element_type=jnp.float32
    )
    d_mixer, d_gate_part, grad_gate = gate_back(d_gated)
    d_y_heads = lax.all_to_all(
        d_mixer.astype(jnp.bfloat16), "seq", split_axis=1, concat_axis=0, tiled=True
    )
    _, ssd_back = jax.vjp(
        ssd_apply, x_float, dt_float, bc_float, bias_local, alog_local, skip_local
    )
    d_x, d_dt, d_bc_part, grad_dtb, grad_alog, grad_skip = ssd_back(d_y_heads.astype(jnp.float32))
    d_bc = lax.psum_scatter(d_bc_part, "seq", scatter_dimension=0, tiled=True)
    d_x_tokens, d_dt_tokens = (
        lax.all_to_all(d_x.astype(jnp.bfloat16), "seq", split_axis=0, concat_axis=1, tiled=True),
        lax.all_to_all(d_dt.astype(jnp.bfloat16), "seq", split_axis=0, concat_axis=1, tiled=True),
    )
    d_conved = jnp.concatenate([d_x_tokens.astype(jnp.float32), d_bc], axis=1)
    d_padded, grad_conv, grad_cbias = conv_back(d_conved)
    rim_grad = shifted(d_padded[: KCONV - 1].astype(jnp.bfloat16), "seq", -1).astype(jnp.float32)
    own_rows = conv_input.shape[0]
    d_conv_input = d_padded[KCONV - 1 :] + jnp.concatenate(
        [jnp.zeros((own_rows - (KCONV - 1), CONVC), jnp.float32), rim_grad], axis=0
    )
    d_projected = jnp.concatenate(
        [d_gate_part, d_conv_input, d_dt_tokens.astype(jnp.float32)], axis=1
    ).astype(jnp.bfloat16)
    grad_in = jnp.einsum("td,tp->dp", normed, d_projected, preferred_element_type=jnp.float32)
    d_normed = lax.dot_general(
        d_projected, full_in, (((1,), (1,)), ((), ())), preferred_element_type=jnp.float32
    )
    d_tokens, grad_norm = rms_back(d_normed)
    d_hidden = (cotangent.astype(jnp.float32) + d_tokens).astype(jnp.bfloat16)
    all_heads = full_dtb.shape[0]
    placed_dtb = lax.dynamic_update_slice_in_dim(
        jnp.zeros((all_heads,), jnp.float32), grad_dtb, head_start, 0
    )
    placed_alog = lax.dynamic_update_slice_in_dim(
        jnp.zeros((all_heads,), jnp.float32), grad_alog, head_start, 0
    )
    placed_skip = lax.dynamic_update_slice_in_dim(
        jnp.zeros((all_heads,), jnp.float32), grad_skip, head_start, 0
    )
    reduced = reduce_grads(
        (
            grad_norm,
            grad_in,
            grad_conv,
            grad_cbias,
            placed_dtb,
            placed_alog,
            placed_skip,
            grad_gate,
            grad_out,
        )
    )
    return (
        layer_out[None],
        d_hidden[None],
        reduced[0],
        reduced[1],
        reduced[2],
        reduced[3],
        reduced[4],
        reduced[5],
        reduced[6],
        reduced[7],
        reduced[8],
    )


f32 = jnp.float32
bf16 = jnp.bfloat16
LANES = 128


def dot(a, b, dims=((1,), (0,))):
    return lax.dot_general(a, b, (dims, ((), ())), preferred_element_type=f32)


def dot_exact(a, b, dims=((1,), (0,))):
    return lax.dot_general(
        a, b, (dims, ((), ())), preferred_element_type=f32, precision=lax.Precision.HIGHEST
    )


def split_dot(a, b, dims=((1,), (0,))):
    high = a.astype(bf16)
    low = (a - high.astype(f32)).astype(bf16)
    return dot(high, b, dims) + dot(low, b, dims)


def iota(shape, axis):
    return lax.broadcasted_iota(jnp.int32, shape, axis)


def spread_matrix(width, head_size):
    return (iota((LANES, width), 1) // head_size == iota((LANES, width), 0)).astype(bf16)


def softplus(v):
    return jnp.maximum(v, 0.0) + jnp.log1p(jnp.exp(-jnp.abs(v)))


def conv_pre(pad_ref, taps, rows):
    total = taps[4:5, :] + pad_ref[5 : 5 + rows, :] * taps[0:1, :]
    for k in range(1, 4):
        total = total + pad_ref[5 + k : 5 + k + rows, :] * taps[k : k + 1, :]
    return total


def scan_forward_kernel(proj_ref, taps_ref, heads_ref, y_ref, core_ref, state_out_ref, pad_ref, state_ref, *, xw, nst, head_size):
    rows = proj_ref.shape[0]
    convw = xw + 2 * nst
    step = pl.program_id(0)

    @pl.when(step == 0)
    def _():
        pad_ref[0:8, :] = jnp.zeros((8, convw), f32)
        state_ref[...] = jnp.zeros(state_ref.shape, f32)

    pad_ref[8 : 8 + rows, :] = proj_ref[:, :convw].astype(f32)
    pre = conv_pre(pad_ref, taps_ref, rows)
    pad_ref[0:8, :] = pad_ref[rows : rows + 8, :]
    conved = (pre * jax.nn.sigmoid(pre)).astype(bf16)
    x = conved[:, :xw].astype(f32)
    b = conved[:, xw : xw + nst]
    c = conved[:, xw + nst :]
    dt = softplus(proj_ref[:, convw:].astype(f32) + heads_ref[0:1, :])
    rate = -jnp.exp(heads_ref[1:2, :]) * dt
    low = iota((rows, rows), 0) >= iota((rows, rows), 1)
    cums = dot_exact(low.astype(f32), rate)
    cums_t = cums.T
    last = cums[rows - 1 : rows, :]
    spread = spread_matrix(xw, head_size)
    wide = split_dot(
        jnp.concatenate([jnp.exp(cums), dt, jnp.exp(last - cums) * dt, jnp.broadcast_to(jnp.exp(last), (8, LANES)), jnp.broadcast_to(heads_ref[2:3, :], (8, LANES))], axis=0),
        spread,
    )
    decay_w = wide[:rows]
    dt_w = wide[rows : 2 * rows]
    tail_w = wide[2 * rows : 3 * rows]
    end_w = wide[3 * rows : 3 * rows + 1]
    skip_w = wide[3 * rows + 8 : 3 * rows + 9]
    state_out_ref[0] = state_ref[...].astype(bf16)
    gram = dot(c, b, ((1,), (1,)))
    xdt = (x * dt_w).astype(bf16)
    first = iota((rows, LANES), 1) < head_size
    diag = []
    per = LANES // head_size
    for pair in range(xw // LANES):
        mats = []
        cols = []
        piece = xdt[:, pair * LANES : (pair + 1) * LANES]
        for j in range(per):
            h = pair * per + j
            gap = jnp.where(low, cums[:, h : h + 1] - cums_t[h : h + 1, :], -1e30)
            mats.append((jnp.exp(gap) * gram).astype(bf16))
            cols.append(jnp.where(first == (j == 0), piece, jnp.zeros_like(piece)))
        diag.append(dot(jnp.concatenate(mats, axis=1), jnp.concatenate(cols, axis=0)))
    inner = jnp.concatenate(diag, axis=1) + dot(c, state_ref[...].astype(bf16)) * decay_w
    y_ref[...] = (inner + x * skip_w).astype(bf16)
    core_ref[...] = inner.astype(core_ref.dtype)
    state_ref[...] = state_ref[...] * end_w + dot(b, (x * tail_w).astype(bf16), ((0,), (0,)))


def scan_forward(proj, taps, heads, xw, nst, head_size, rows=128, core_dtype=f32):
    total = proj.shape[0]
    convw = xw + 2 * nst
    steps = total // rows
    return pl.pallas_call(
        functools.partial(scan_forward_kernel, xw=xw, nst=nst, head_size=head_size),
        grid=(steps,),
        in_specs=[
            pl.BlockSpec((rows, proj.shape[1]), lambda i: (i, 0)),
            pl.BlockSpec(taps.shape, lambda i: (0, 0)),
            pl.BlockSpec(heads.shape, lambda i: (0, 0)),
        ],
        out_specs=[
            pl.BlockSpec((rows, xw), lambda i: (i, 0)),
            pl.BlockSpec((rows, xw), lambda i: (i, 0)),
            pl.BlockSpec((1, nst, xw), lambda i: (i, 0, 0)),
        ],
        out_shape=[
            jax.ShapeDtypeStruct((total, xw), bf16),
            jax.ShapeDtypeStruct((total, xw), core_dtype),
            jax.ShapeDtypeStruct((steps, nst, xw), bf16),
        ],
        scratch_shapes=[pltpu.VMEM((rows + 8, convw), f32), pltpu.VMEM((nst, xw), f32)],
        name="scan_forward",
    )(proj, taps, heads)


def scan_backward_kernel(proj_ref, halo_ref, taps_ref, heads_ref, dy_ref, core_ref, state_in_ref, dproj_ref, chan_ref, head_ref, pad_ref, grad_ref, dpre_ref, *, xw, nst, head_size):
    rows = proj_ref.shape[0]
    convw = xw + 2 * nst
    step = pl.program_id(0)
    steps = pl.num_programs(0)

    @pl.when(step == 0)
    def _():
        grad_ref[...] = jnp.zeros(grad_ref.shape, f32)
        dpre_ref[rows : rows + 8, :] = jnp.zeros((8, convw), f32)
        chan_ref[...] = jnp.zeros(chan_ref.shape, f32)
        head_ref[...] = jnp.zeros(head_ref.shape, f32)

    halo = halo_ref[8:16, :convw].astype(f32)
    pad_ref[0:8, :] = jnp.where(step == steps - 1, jnp.zeros_like(halo), halo)
    pad_ref[8 : 8 + rows, :] = proj_ref[:, :convw].astype(f32)
    pre = conv_pre(pad_ref, taps_ref, rows)
    sig = jax.nn.sigmoid(pre)
    conved = (pre * sig).astype(bf16)
    slope = sig * (1.0 + pre * (1.0 - sig))
    x = conved[:, :xw].astype(f32)
    b = conved[:, xw : xw + nst]
    c = conved[:, xw + nst :]
    raw = proj_ref[:, convw:].astype(f32) + heads_ref[0:1, :]
    dt = softplus(raw)
    speed = -jnp.exp(heads_ref[1:2, :])
    rate = speed * dt
    low = iota((rows, rows), 0) >= iota((rows, rows), 1)
    up = iota((rows, rows), 0) <= iota((rows, rows), 1)
    cums = dot_exact(low.astype(f32), rate)
    cums_t = cums.T
    last = cums[rows - 1 : rows, :]
    spread = spread_matrix(xw, head_size)
    wide = split_dot(
        jnp.concatenate([jnp.exp(cums), dt, jnp.exp(last - cums), jnp.broadcast_to(jnp.exp(last), (8, LANES)), jnp.broadcast_to(heads_ref[2:3, :], (8, LANES))], axis=0),
        spread,
    )
    decay_w = wide[:rows]
    dt_w = wide[rows : 2 * rows]
    tail_w = wide[2 * rows : 3 * rows]
    end_w = wide[3 * rows : 3 * rows + 1]
    skip_w = wide[3 * rows + 8 : 3 * rows + 9]
    dy16 = dy_ref[...]
    dy = dy16.astype(f32)
    gram_t = dot(b, c, ((1,), (1,)))
    xdt_f = x * dt_w
    xdt = xdt_f.astype(bf16)
    first = iota((rows, LANES), 1) < head_size
    per = LANES // head_size
    dgram_t = jnp.zeros((rows, rows), f32)
    diag = []
    for pair in range(xw // LANES):
        mats = []
        cols = []
        piece = xdt[:, pair * LANES : (pair + 1) * LANES]
        dpiece = dy16[:, pair * LANES : (pair + 1) * LANES]
        for j in range(per):
            h = pair * per + j
            keep = first == (j == 0)
            gap = jnp.where(up, cums_t[h : h + 1, :] - cums[:, h : h + 1], -1e30)
            factor = jnp.exp(gap)
            mats.append((factor * gram_t).astype(bf16))
            cols.append(jnp.where(keep, dpiece, jnp.zeros_like(dpiece)))
            dmix = dot(jnp.where(keep, piece, jnp.zeros_like(piece)), dpiece, ((1,), (1,)))
            dgram_t = dgram_t + dmix * factor
        diag.append(dot(jnp.concatenate(mats, axis=1), jnp.concatenate(cols, axis=0)))
    grad16 = grad_ref[...].astype(bf16)
    outer = dot(b, grad16) * tail_w
    unit = jnp.concatenate(diag, axis=1) + outer
    dx = unit * dt_w + skip_w * dy
    dydec = (dy * decay_w).astype(bf16)
    state16 = state_in_ref[0]
    dgram16 = dgram_t.astype(bf16)
    db = dot(dgram16, c) + dot((xdt_f * tail_w).astype(bf16), grad16, ((1,), (1,)))
    dc = dot(dgram16, b, ((0,), (0,))) + dot(dydec, state16, ((1,), (1,)))
    xdt_r = xdt.astype(f32)
    carried = grad_ref[...] * end_w
    edge = jnp.sum(outer * xdt_r, axis=0, keepdims=True) + jnp.sum(
        carried * state16.astype(f32), axis=0, keepdims=True
    )
    sums = split_dot(
        jnp.concatenate(
            [
                unit * x,
                dy * core_ref[...] - unit * xdt_r,
                jnp.broadcast_to(edge, (8, xw)),
                jnp.broadcast_to(jnp.sum(dy * x, axis=0, keepdims=True), (8, xw)),
            ],
            axis=0,
        ),
        spread,
        ((1,), (1,)),
    )
    direct = sums[:rows]
    dcums = sums[rows : 2 * rows] + jnp.where(
        iota((rows, LANES), 0) == rows - 1, sums[2 * rows : 2 * rows + 1], 0.0
    )
    drate = dot_exact(up.astype(f32), dcums)
    draw = (direct + speed * drate) * jax.nn.sigmoid(raw)
    head_ref[0:1, :] += jnp.sum(draw, axis=0, keepdims=True)
    head_ref[1:2, :] += jnp.sum(drate * rate, axis=0, keepdims=True)
    head_ref[2:3, :] += sums[2 * rows + 8 : 2 * rows + 9]
    grad_ref[...] = carried + dot(c, dydec, ((0,), (0,)))
    dconv = jnp.concatenate([dx.astype(bf16).astype(f32), db, dc], axis=1)
    dpre = dconv * slope
    dpre_ref[0:rows, :] = dpre
    din = dpre_ref[0:rows, :] * taps_ref[3:4, :]
    for k in range(3):
        din = din + dpre_ref[3 - k : 3 - k + rows, :] * taps_ref[k : k + 1, :]
    dproj_ref[:, :convw] = din.astype(bf16)
    dproj_ref[:, convw:] = draw.astype(bf16)
    for k in range(4):
        chan_ref[k : k + 1, :] += jnp.sum(dpre * pad_ref[5 + k : 5 + k + rows, :], axis=0, keepdims=True)
    chan_ref[4:5, :] += jnp.sum(dpre, axis=0, keepdims=True)
    dpre_ref[rows : rows + 8, :] = dpre[0:8, :]


def scan_backward(proj, taps, heads, dy, core, states, xw, nst, head_size, rows=128):
    total = proj.shape[0]
    convw = xw + 2 * nst
    steps = total // rows
    back = lambda i: (steps - 1 - i, 0)
    return pl.pallas_call(
        functools.partial(scan_backward_kernel, xw=xw, nst=nst, head_size=head_size),
        grid=(steps,),
        in_specs=[
            pl.BlockSpec((rows, proj.shape[1]), back),
            pl.BlockSpec((16, proj.shape[1]), lambda i: (jnp.maximum((steps - 1 - i) * (rows // 16) - 1, 0), 0)),
            pl.BlockSpec(taps.shape, lambda i: (0, 0)),
            pl.BlockSpec(heads.shape, lambda i: (0, 0)),
            pl.BlockSpec((rows, xw), back),
            pl.BlockSpec((rows, xw), back),
            pl.BlockSpec((1, nst, xw), lambda i: (steps - 1 - i, 0, 0)),
        ],
        out_specs=[
            pl.BlockSpec((rows, proj.shape[1]), back),
            pl.BlockSpec((8, convw), lambda i: (0, 0)),
            pl.BlockSpec((8, LANES), lambda i: (0, 0)),
        ],
        out_shape=[
            jax.ShapeDtypeStruct(proj.shape, bf16),
            jax.ShapeDtypeStruct((8, convw), f32),
            jax.ShapeDtypeStruct((8, LANES), f32),
        ],
        scratch_shapes=[
            pltpu.VMEM((rows + 8, convw), f32),
            pltpu.VMEM((nst, xw), f32),
            pltpu.VMEM((rows + 8, convw), f32),
        ],
        name="scan_backward",
    )(proj, proj, taps, heads, dy, core, states)


def gather_direct(x, axis, n):
    i = lax.axis_index(axis)
    whole = lax.dynamic_update_index_in_dim(jnp.zeros((n,) + x.shape, x.dtype), x, i, 0)
    for m in range(1, n):
        got = lax.ppermute(x, axis, [(s, (s + m) % n) for s in range(n)])
        whole = lax.dynamic_update_index_in_dim(whole, got, (i - m) % n, 0)
    return whole


def scatter_sum_direct(parts, axis, n):
    i = lax.axis_index(axis)
    total = lax.dynamic_index_in_dim(parts, i, 0, keepdims=False)
    for m in range(1, n):
        block = lax.dynamic_index_in_dim(parts, (i + m) % n, 0, keepdims=False)
        got = lax.ppermute(block.astype(bf16), axis, [(s, (s + m) % n) for s in range(n)])
        total = total + got.astype(f32)
    return total


def sum_direct(x, axis, n):
    total = x
    for m in range(1, n):
        total = total + lax.ppermute(x, axis, [(s, (s + m) % n) for s in range(n)])
    return total


def line_gather(x, axis, n):
    i = lax.axis_index(axis)
    ups = [x]
    downs = [x]
    for k in range(1, n):
        ups.append(lax.ppermute(ups[-1], axis, [(j, j + 1) for j in range(k - 1, n - 1)]))
        downs.append(lax.ppermute(downs[-1], axis, [(j + 1, j) for j in range(n - k)]))
    whole = lax.dynamic_update_index_in_dim(jnp.zeros((n,) + x.shape, x.dtype), x, i, 0)
    for k in range(1, n):
        piece = jnp.where(i >= k, ups[k], downs[n - k])
        whole = lax.dynamic_update_index_in_dim(whole, piece, (i - k) % n, 0)
    return whole


def line_scatter_sum(parts, axis, n):
    i = lax.axis_index(axis)

    def own(index):
        return lax.dynamic_index_in_dim(parts, jnp.clip(index, 0, n - 1), 0, keepdims=False)

    up = None
    down = None
    for k in range(1, n):
        send_up = own(n - k + i)
        send_down = own(i + k - n)
        if k > 1:
            send_up = send_up.astype(f32) + up.astype(f32)
            send_down = send_down.astype(f32) + down.astype(f32)
        up = lax.ppermute(send_up.astype(bf16), axis, [(j, j + 1) for j in range(min(k, n - 1))])
        down = lax.ppermute(
            send_down.astype(bf16), axis, [(n - 1 - j, n - 2 - j) for j in range(min(k, n - 1))]
        )
    return own(i).astype(f32) + up.astype(f32) + down.astype(f32)


def core_join(x, n):
    if n == 1:
        return x[None]
    return gather_direct(x, "grp", n)


def head_parallel_body(
    hidden,
    norm_gain,
    in_weight,
    conv_weight,
    conv_bias,
    dt_bias,
    a_log,
    skip_gain,
    gate_gain,
    out_weight,
    d_out,
    sizes,
):
    nseq, ngrp, nwsh = sizes
    s = lax.axis_index("seq")
    z = lax.axis_index("wsh")
    core = lax.axis_index("grp")
    own_rows, width = hidden.shape[1:]
    length = own_rows * nseq
    taps = conv_weight.shape[1]
    inner = gate_gain.shape[0] * nwsh
    channels = conv_bias.shape[0] * nwsh
    heads = dt_bias.shape[0] * nwsh
    head_size = inner // heads
    bc = channels - inner
    states = bc // 2
    zin = inner // nwsh
    part = zin // nseq
    local = inner // nseq
    zheads = heads // nwsh
    hpart = zheads // nseq
    lheads = heads // nseq
    convw = local + bc

    def pick(w, base, block, piece):
        cuts = [
            lax.dynamic_slice_in_dim(w, base + k * block + s * piece, piece, axis=1)
            for k in range(nwsh)
        ]
        return jnp.concatenate(cuts, axis=1)

    def halves(x):
        rows = x.shape[0] // ngrp
        return lax.dynamic_slice_in_dim(x, core * rows, rows, axis=0)

    scan_cols = jnp.concatenate(
        [
            pick(in_weight, inner, zin, part),
            in_weight[:, 2 * inner : 2 * inner + bc],
            pick(in_weight, inner + channels, zheads, hpart),
            jnp.zeros((in_weight.shape[0], LANES - lheads), bf16),
        ],
        axis=1,
    )
    gate_cols = pick(in_weight, 0, zin, part)
    out_rows = lax.dynamic_slice_in_dim(out_weight, s * part, part, axis=0)

    small = jnp.concatenate(
        [
            norm_gain,
            conv_weight.T.reshape(-1),
            conv_bias,
            dt_bias,
            a_log,
            skip_gain,
            gate_gain,
        ]
    )
    small_len = small.shape[0]
    small = jnp.pad(small, (0, -small_len % 2048)).reshape(-1, LANES)
    small = gather_direct(small, "wsh", nwsh).reshape(nwsh, -1)
    tokens = gather_direct(hidden[0], "seq", nseq).reshape(length, width)

    def weight_gather(x):
        got = core_join(line_gather(halves(x), "wsh", nwsh), ngrp)
        return jnp.swapaxes(got, 0, 1).reshape(nwsh * x.shape[0], x.shape[1])

    w_scan = weight_gather(scan_cols)
    w_gate = weight_gather(gate_cols)
    w_out = weight_gather(out_rows)
    cot = gather_direct(d_out[0], "seq", nseq).reshape(length, width)

    at = 0

    def take(count):
        nonlocal at
        piece = small[:, at : at + count]
        at += count
        return piece

    zch = conv_bias.shape[0]
    full_norm = take(norm_gain.shape[0]).reshape(-1).astype(f32)
    full_taps = jnp.swapaxes(take(zch * taps).reshape(nwsh, taps, zch), 0, 1).reshape(taps, channels)
    full_cbias = take(zch).reshape(1, channels)
    head_rows = [take(zheads) for _ in range(3)]
    full_gain = take(zin)

    def local_heads(x):
        return lax.dynamic_slice_in_dim(x, s * hpart, hpart, axis=1).reshape(1, lheads)

    head_par = jnp.concatenate([local_heads(x) for x in head_rows], axis=0).astype(f32)
    head_par = jnp.pad(head_par, ((0, 5), (0, LANES - lheads)))
    gain = lax.dynamic_slice_in_dim(full_gain, s * part, part, axis=1).reshape(local).astype(f32)
    chan = jnp.concatenate([full_taps, full_cbias], axis=0)
    chan_par = jnp.concatenate([pick(chan, 0, zin, part), chan[:, inner:]], axis=1).astype(f32)
    chan_par = jnp.pad(chan_par, ((0, 8 - taps - 1), (0, 0)))

    tok_f = tokens.astype(f32)
    inv_in = lax.rsqrt(jnp.mean(tok_f * tok_f, axis=-1, keepdims=True) + epsilon)
    normed = (tok_f * inv_in * full_norm[None]).astype(bf16)
    proj = dot(normed, w_scan).astype(bf16)
    y16, core_y, states_in = scan_forward(proj, chan_par, head_par, local, states, head_size)
    gate16 = dot(normed, w_gate).astype(bf16)
    d_gated = dot(cot, w_out, ((1,), (1,)))
    y = y16.astype(f32)
    gate = gate16.astype(f32)
    sig = jax.nn.sigmoid(gate)
    product = y * (gate * sig)
    dg = d_gated * gain[None]
    sums = jnp.stack([jnp.sum(product * product, axis=1), jnp.sum(dg * product, axis=1)])
    sums = sum_direct(sums, "seq", nseq)
    inv = lax.rsqrt(sums[0] / inner + epsilon)[:, None]
    pull = (sums[1] / inner)[:, None] * inv * inv
    normal = product * inv
    gated = (normal * gain[None]).astype(bf16)
    out_part = dot(gated, w_out).reshape(nseq, own_rows, width)
    layer_out = (hidden[0].astype(f32) + scatter_sum_direct(out_part, "seq", nseq)).astype(bf16)
    grad_out = dot(gated, cot, ((0,), (0,)))
    d_product = inv * (dg - product * pull)
    grad_gain = jnp.sum(d_gated * normal, axis=0)
    d_y = (d_product * (gate * sig)).astype(bf16)
    d_gate = (d_product * y * (sig * (1.0 + gate * (1.0 - sig)))).astype(bf16)

    d_proj, chan_grad, head_grad = scan_backward(
        proj, chan_par, head_par, d_y, core_y, states_in, local, states, head_size
    )
    grad_gate_cols = dot(normed, d_gate, ((0,), (0,)))
    grad_scan_cols = dot(normed, d_proj, ((0,), (0,)))
    d_normed = dot(d_gate, w_gate, ((1,), (1,))) + dot(d_proj, w_scan, ((1,), (1,)))
    grad_norm = jnp.sum(d_normed * (tok_f * inv_in), axis=0)

    own_f = hidden[0].astype(f32)
    d_normed_own = scatter_sum_direct(d_normed.reshape(nseq, own_rows, width), "seq", nseq)
    own_inv = lax.rsqrt(jnp.mean(own_f * own_f, axis=-1, keepdims=True) + epsilon)
    pulled = d_normed_own * full_norm[None]
    d_tokens = own_inv * (
        pulled
        - own_f * (own_inv * own_inv * jnp.mean(pulled * own_f, axis=-1, keepdims=True))
    )
    d_hidden = (d_out[0].astype(f32) + d_tokens).astype(bf16)

    def reduce_weight(g):
        rows, cols = g.shape
        half = rows // (nwsh * ngrp)
        g = jnp.swapaxes(g.reshape(nwsh, ngrp, half, cols), 0, 1)
        mine = scatter_sum_direct(g, "grp", ngrp).astype(bf16)
        done = line_scatter_sum(mine, "wsh", nwsh).astype(bf16)
        got = gather_direct(done, "seq", nseq)
        return core_join(got, ngrp)

    def columns(g):
        return jnp.swapaxes(g, 0, 1).reshape(nseq, -1, g.shape[-1]).astype(f32)

    out_all = jnp.swapaxes(reduce_weight(grad_out), 0, 1)
    grad_out_weight = out_all.reshape(zin, width).astype(f32)
    gate_all = columns(reduce_weight(grad_gate_cols))
    scan_all = columns(reduce_weight(grad_scan_cols))

    def unpick(g, piece):
        rows = g.shape[1]
        g = g.reshape(nseq, rows, nwsh, piece)
        return jnp.transpose(g, (1, 2, 0, 3)).reshape(rows, nwsh * nseq * piece)

    grad_in = jnp.concatenate(
        [
            unpick(gate_all, part),
            unpick(scan_all[:, :, :local], part),
            jnp.sum(scan_all[:, :, local:convw], axis=0),
            unpick(scan_all[:, :, convw : convw + lheads], hpart),
        ],
        axis=1,
    )

    small_grads = jnp.concatenate(
        [
            grad_gain,
            chan_grad[: taps + 1].reshape(-1),
            head_grad[:3, :lheads].reshape(-1),
            grad_norm,
        ]
    )
    count = small_grads.shape[0]
    small_grads = jnp.pad(small_grads, (0, -count % 1024)).reshape(-1, LANES)
    small_grads = sum_direct(small_grads, "grp", ngrp)
    small_grads = sum_direct(small_grads, "wsh", nwsh)
    small_grads = gather_direct(small_grads, "seq", nseq).reshape(nseq, -1)
    at = 0

    def take_grad(count):
        nonlocal at
        piece = small_grads[:, at : at + count]
        at += count
        return piece

    def shard(x, axis=0):
        size = x.shape[axis] // nwsh
        return lax.dynamic_slice_in_dim(x, z * size, size, axis=axis)

    gain_all = take_grad(local)[:, None, :]
    chan_all = take_grad((taps + 1) * convw).reshape(nseq, taps + 1, convw)
    head_all = take_grad(3 * lheads).reshape(nseq, 3, lheads)
    norm_all = jnp.sum(take_grad(width), axis=0)
    grad_gate_gain = shard(unpick(gain_all, part)[0])
    chan_full = jnp.concatenate(
        [unpick(chan_all[:, :, :local], part), jnp.sum(chan_all[:, :, local:], axis=0)], axis=1
    )
    head_full = unpick(head_all, hpart)
    chan_own = shard(chan_full, 1)
    head_own = shard(head_full, 1)
    return (
        layer_out[None],
        d_hidden[None],
        shard(norm_all),
        grad_in,
        chan_own[:taps].T,
        chan_own[taps],
        head_own[0],
        head_own[1],
        head_own[2],
        grad_gate_gain,
        grad_out_weight,
    )


def body(*args, sizes):
    nseq, ngrp, nwsh = sizes
    zheads = args[5].shape[0]
    if zheads % nseq or nseq == 1 or nwsh == 1:
        return token_parallel_body(*args)
    return head_parallel_body(*args, sizes)


def solution(mesh):
    placed = (
        P(("grp", "wsh"), "seq", None),
        P("wsh"),
        P("wsh", None),
        P("wsh", None),
        P("wsh"),
        P("wsh"),
        P("wsh"),
        P("wsh"),
        P("wsh"),
        P("wsh", None),
        P(("grp", "wsh"), "seq", None),
    )
    shape = mesh.shape
    return jax.shard_map(
        functools.partial(body, sizes=(shape["seq"], shape["grp"], shape["wsh"])),
        mesh=mesh,
        in_specs=placed,
        out_specs=(
            P(("grp", "wsh"), "seq", None),
            P(("grp", "wsh"), "seq", None),
            P("wsh"),
            P("wsh", None),
            P("wsh", None),
            P("wsh"),
            P("wsh"),
            P("wsh"),
            P("wsh"),
            P("wsh"),
            P("wsh", None),
        ),
        check_vma=False,
    )
```
